32 devices in a mesh: rows: 8 (over y, x, core), feat: 4 (over z).
Axes of the slice: x: 2, y: 2, z: 4, core: 2. Of those that a mesh axis runs over, the one named last changes fastest.
Arguments:
- queries: bfloat16 [49152, 4096], P('rows', 'feat'), may hold values from -6 to 6
- projection: bfloat16 [4096, 128], P('feat'), may hold values from -0.09375 to 0.09375
- models: float32 [64, 128], replicated, may hold values from -0.5 to 0.5
- first: int32 [49152], P('rows'), may hold values from 0 to 63
- second: int32 [49152], P('rows'), may hold values from 0 to 63
- wins: int32 [49152], P('rows'), may hold values 0 or 1
Outputs:
- update_proj: float32 [4096, 128], P('feat')
- update_models: float32 [64, 128], replicated
- loss: float32 [], replicated
The draws below stay inside these ranges and needn't reach their ends.
All inputs are finite; a program needn't handle non-finite values. No bound on the sum of `wins` on one device may be relied on, other than what follows from the above.
Results may differ from the reference program's by a relative error of at most 0.00045.
The reference program's roundings to bfloat16 on the way (of `back`) count: a program that leaves them out, or rounds other values in their place, can miss the bound.
Values may be sent and summed in bfloat16 or wider, within the bound.
A program may use at most 64 MiB of HBM per device.

```python
import jax
import jax.numpy as jnp
from jax import lax

D = 4096
R = 128
NM = 64
TOKENS = 49152


def touch_ends(array, own_key, smallest, high):
    longest = array.shape.index(max(array.shape))
    spots = []
    for shift in (0, 1):
        where = [jax.random.randint(jax.random.fold_in(own_key, axis), (), 0, length) for axis, length in enumerate(array.shape)]
        where[longest] = (where[longest] + shift) % array.shape[longest]
        spots.append(tuple(where))
    return array.at[spots[0]].set(smallest).at[spots[1]].set(high)


def levels(stream_key, dims, cuts, low, largest):
    gain, own = 1.0, jax.random.fold_in(stream_key, 6)
    for axis_at, blocks in cuts:
        draws = jnp.exp(jax.random.uniform(jax.random.fold_in(own, axis_at), (blocks,), jnp.float32, low / len(cuts), largest / len(cuts)))
        gain = gain * jnp.repeat(draws, dims[axis_at] // blocks).reshape([-1 if axis == axis_at else 1 for axis in range(len(dims))])
    return gain


def scatter_about(own_key, shape, scale, limit, split=(), kind=jnp.bfloat16):
    entries = jax.random.normal(own_key, shape, jnp.float32) * scale
    if len(split) > 0:
        entries = levels(own_key, shape, split, -0.22, 0.18) * entries
    return jnp.clip(entries, min=-limit, max=limit).astype(kind)


def setup_inputs(seed: int = 0) -> dict:
    keys = jax.random.split(jax.random.key(seed), 7)
    queries = scatter_about(keys[0], (TOKENS, D), 1.0, 6.0, ((0, 8), (1, 4)))
    projection = scatter_about(keys[1], (D, R), D ** -0.5, 0.09375, ((0, 4),))
    models = scatter_about(keys[2], (NM, R), R ** -0.5, 0.5, (), jnp.float32)
    first = touch_ends(jax.random.randint(keys[3], (TOKENS,), 0, NM), jax.random.fold_in(keys[3], 1), 0, NM - 1).astype(jnp.int32)
    second = touch_ends(jax.random.randint(keys[4], (TOKENS,), 0, NM), jax.random.fold_in(keys[4], 1), 0, NM - 1).astype(jnp.int32)
    wins = touch_ends((jax.random.randint(keys[5], (TOKENS,), 0, 2) < 1).astype(jnp.int32), jax.random.fold_in(keys[5], 1), 0, 1)
    return {"queries": queries, "projection": projection, "models": models, "first": first, "second": second, "wins": wins}


def reference(queries, projection, models, first, second, wins):
    routed = jnp.dot(queries, projection, preferred_element_type=jnp.float32)
    gap = jnp.take(models, first, axis=0) - jnp.take(models, second, axis=0)
    margin = lax.optimization_barrier(jnp.sum(routed * gap, axis=-1))
    sign = 2.0 * wins.astype(jnp.float32) - 1.0
    loss = jnp.sum(jax.nn.softplus(-sign * margin)) / TOKENS
    coef = -sign * jax.nn.sigmoid(-sign * margin) / TOKENS
    back = (coef[:, None] * gap).astype(jnp.bfloat16)
    grad_proj = jnp.dot(queries.T, back, preferred_element_type=jnp.float32)
    labels = jnp.arange(NM, dtype=jnp.int32)[:, None]
    pick = (labels == first[None, :]).astype(jnp.float32) - (labels == second[None, :]).astype(jnp.float32)
    grad_models = jnp.dot(pick, coef[:, None] * routed, precision=lax.Precision.HIGHEST)
    total = jnp.sum(grad_proj * grad_proj) + jnp.sum(grad_models * grad_models)
    scale = jnp.sqrt(jnp.float32(D * R + NM * R)) / (jnp.sqrt(total) + 1e-06)
    return (scale * grad_proj, scale * grad_models, loss)
```

```python
import functools

import jax
import jax.numpy as jnp
from jax import lax
from jax.experimental import pallas as pl
from jax.experimental.pallas import tpu as pltpu
from jax.sharding import PartitionSpec as P

F32 = jnp.float32
BF16 = jnp.bfloat16
SUB = 256
MESH = pl.DeviceIdType.MESH
NT = (((1,), (1,)), ((), ()))


def dot_nt(a, b):
    return lax.dot_general(a, b, NT, preferred_element_type=F32)


def split3(x):
    hi = x.astype(BF16)
    rest = x - hi.astype(F32)
    mid = rest.astype(BF16)
    lo = (rest - mid.astype(F32)).astype(BF16)
    return hi, mid, lo


def kernel(
    nrows, nfeat, chunks, blocks, total_dim,
    q_hbm, proj_ref, models_ref, first_ref, second_ref, wins_ref,
    out_ref, um_ref, loss_ref,
    qv, gap_v, routed_v, back_v, pick_v, marg, gblk, prt, csum, rbuf, gfull,
    mbuf, mprt, mrow, mfeat, mtot, sqf, sqr,
    q_sem, mg_s, mg_r, pr_s, pr_r, rs_s, rs_r, ag_s, ag_r, fw_s, fw_r,
    ma_s, ma_r, mb_s, mb_r, mc_s, mc_r, md_s, md_r, sf_s, sf_r, sr_s, sr_r,
):
    row = lax.axis_index("rows")
    feat = lax.axis_index("feat")
    core = lax.rem(row, 2)
    chip = lax.div(row, 2)
    chips = nrows // 2
    partner = chip * 2 + (1 - core)
    tokens, dloc = qv.shape
    rdim = proj_ref.shape[1]
    nm = models_ref.shape[0]
    t = tokens // chunks
    bw = dloc // blocks
    half = bw // 2
    fs = dloc // nrows
    gpb = half // fs
    mh = mbuf.shape[0] // 2
    total_rows = float(tokens * nrows)

    def qcopy(c):
        at = pl.ds(c * t, t)
        return pltpu.make_async_copy(q_hbm.at[at], qv.at[at], q_sem.at[c])

    for c in range(chunks):
        qcopy(c).start()

    barrier = pltpu.get_barrier_semaphore()
    for d in range(1, nfeat):
        pl.semaphore_signal(
            barrier, inc=1, device_id=(row, lax.rem(feat + d, nfeat)), device_id_type=MESH
        )
    for d in range(1, nrows):
        pl.semaphore_signal(
            barrier, inc=1, device_id=(lax.rem(row + d, nrows), feat), device_id_type=MESH
        )

    def remote(src, dst, send, recv, to_row, to_feat):
        return pltpu.make_async_remote_copy(
            src_ref=src, dst_ref=dst, send_sem=send, recv_sem=recv,
            device_id=(to_row, to_feat), device_id_type=MESH,
        )

    sent = []

    def push(*args):
        cp = remote(*args)
        cp.start()
        sent.append(cp)

    def arrived(dst, send, recv):
        remote(dst, dst, send, recv, partner, feat).wait_recv()

    eye = (
        lax.broadcasted_iota(jnp.int32, (rdim, rdim), 0)
        == lax.broadcasted_iota(jnp.int32, (rdim, rdim), 1)
    ).astype(F32).astype(BF16)
    proj_t = dot_nt(eye, proj_ref[...]).astype(BF16)
    models3 = jnp.concatenate(split3(models_ref[...]), axis=0)
    models3_t = dot_nt(eye, models3).astype(BF16)

    label = lax.broadcasted_iota(jnp.int32, (nm, SUB), 0)
    for s in range(tokens // SUB):
        at = pl.ds(s * SUB, SUB)
        pick = (
            (label == first_ref[:, at]).astype(F32) - (label == second_ref[:, at]).astype(F32)
        ).astype(BF16)
        pick_v[:, at] = pick
        pick3 = jnp.concatenate([pick, pick, pick], axis=0)
        gap_v[:, at] = jnp.dot(models3_t, pick3, preferred_element_type=F32)

    pl.semaphore_wait(barrier, nfeat - 1 + nrows - 1)

    for c in range(chunks):
        qcopy(c).wait()
        for s in range(t // SUB):
            at = pl.ds(c * t + s * SUB, SUB)
            routed = dot_nt(proj_t, qv[at, :])
            routed_v[:, at] = routed
            marg[feat, c, :, pl.ds(s * SUB, SUB)] = jnp.sum(
                routed * gap_v[:, at], axis=0, keepdims=True
            )
        for d in range(1, nfeat):
            push(
                marg.at[feat, c], marg.at[feat, c], mg_s.at[c, d], mg_r.at[c, feat],
                row, lax.rem(feat + d, nfeat),
            )

    loss_row = jnp.zeros((1, t), F32)
    msum = jnp.zeros((nm, 2 * rdim), F32)
    for c in range(chunks):
        for d in range(1, nfeat):
            frm = lax.rem(feat + d, nfeat)
            arrived(marg.at[frm, c], mg_s.at[c, d], mg_r.at[c, frm])
        at = pl.ds(c * t, t)
        margin = marg[0, c]
        for z in range(1, nfeat):
            margin = margin + marg[z, c]
        sign = 2.0 * wins_ref[:, at].astype(F32) - 1.0
        x = -sign * margin
        loss_row = loss_row + (jnp.maximum(x, 0.0) + jnp.log1p(jnp.exp(-jnp.abs(x))))
        coef = -sign * jax.nn.sigmoid(x) / total_rows
        for s in range(t // SUB):
            sub = pl.ds(c * t + s * SUB, SUB)
            cs = coef[:, s * SUB:(s + 1) * SUB]
            back_v[:, sub] = (cs * gap_v[:, sub]).astype(BF16)
            w = cs * routed_v[:, sub]
            hi = w.astype(BF16)
            lo = (w - hi.astype(F32)).astype(BF16)
            msum = msum + dot_nt(pick_v[:, sub], jnp.concatenate([hi, lo], axis=0))

    mbuf[0:nm, :] = msum[:, :rdim] + msum[:, rdim:]
    lsum = loss_row[:, 0:rdim]
    for i in range(1, t // rdim):
        lsum = lsum + loss_row[:, i * rdim:(i + 1) * rdim]
    tail = mbuf.shape[0] - nm
    mbuf[nm:, :] = jnp.where(
        lax.broadcasted_iota(jnp.int32, (tail, rdim), 0) == 0,
        jnp.broadcast_to(lsum, (tail, rdim)), 0.0,
    )
    push(mbuf.at[pl.ds((1 - core) * mh, mh)], mprt, ma_s, ma_r, partner, feat)

    def block_of(i):
        return lax.rem(lax.div(chip, gpb) + 1 + i, blocks)

    def block_grad(i):
        cols = pl.ds(pl.multiple_of(block_of(i) * bw, 128), bw)
        acc = jnp.zeros((rdim, bw), F32)
        for c in range(chunks):
            at = pl.ds(c * t, t)
            acc = acc + jnp.dot(back_v[:, at], qv[at, cols], preferred_element_type=F32)
        gblk[i] = acc.T
        push(
            gblk.at[i, pl.ds((1 - core) * half, half)], prt.at[i], pr_s.at[i], pr_r.at[i],
            partner, feat,
        )

    kept = []

    def chip_sum(i):
        arrived(prt.at[i], pr_s.at[i], pr_r.at[i])
        csum[i] = gblk[i, pl.ds(core * half, half), :] + prt[i]
        for j in range(gpb):
            to = block_of(i) * gpb + j
            if gpb == 1 and i == blocks - 1:
                rbuf[chip] = csum[i, pl.ds(j * fs, fs), :]
                continue
            cp = remote(
                csum.at[i, pl.ds(j * fs, fs)], rbuf.at[chip], rs_s.at[i, j], rs_r.at[chip],
                to * 2 + core, feat,
            )
            if gpb == 1:
                cp.start()
                sent.append(cp)
            else:
                @pl.when(to != chip)
                def _():
                    cp.start()

                @pl.when(to == chip)
                def _():
                    rbuf[chip] = csum[i, pl.ds(j * fs, fs), :]

                kept.append((to, cp))

    block_grad(0)
    arrived(mprt, ma_s, ma_r)
    mrow[chip] = mbuf[pl.ds(core * mh, mh), :] + mprt[...]
    for d in range(1, chips):
        push(
            mrow.at[chip], mrow.at[chip], mb_s.at[d], mb_r.at[chip],
            lax.rem(chip + d, chips) * 2 + core, feat,
        )
    for i in range(1, blocks):
        block_grad(i)
        chip_sum(i - 1)
    for d in range(1, chips):
        frm = lax.rem(chip + d, chips)
        arrived(mrow.at[frm], mb_s.at[d], mb_r.at[frm])
    mr = mrow[0]
    for i in range(1, chips):
        mr = mr + mrow[i]
    mfeat[feat] = mr
    for d in range(1, nfeat):
        push(
            mfeat.at[feat], mfeat.at[feat], mc_s.at[d], mc_r.at[feat],
            row, lax.rem(feat + d, nfeat),
        )
    chip_sum(blocks - 1)

    def offset(c, k):
        return pl.multiple_of(lax.div(c, gpb) * bw + k * half + lax.rem(c, gpb) * fs, 8)

    def slice_of(c, k):
        return gfull.at[pl.ds(offset(c, k), fs)]

    for d in range(1, chips):
        frm = lax.rem(chip + d, chips)
        arrived(rbuf.at[frm], ag_s.at[d], rs_r.at[frm])
    own = rbuf[0]
    for i in range(1, chips):
        own = own + rbuf[i]
    gfull[pl.ds(offset(chip, core), fs), :] = own
    for d in range(1, chips):
        push(
            slice_of(chip, core), slice_of(chip, core), ag_s.at[d], ag_r.at[chip],
            lax.rem(chip + d, chips) * 2 + core, feat,
        )
    push(
        slice_of(chip, core), slice_of(chip, core), fw_s.at[0], fw_r.at[chip], partner, feat
    )
    square = own * own
    sq = square[0:8]
    for i in range(1, fs // 8):
        sq = sq + square[i * 8:(i + 1) * 8]
    sqf[feat] = sq
    for d in range(1, nfeat):
        push(
            sqf.at[feat], sqf.at[feat], sf_s.at[d], sf_r.at[feat],
            row, lax.rem(feat + d, nfeat),
        )

    for d in range(1, nfeat):
        frm = lax.rem(feat + d, nfeat)
        arrived(mfeat.at[frm], mc_s.at[d], mc_r.at[frm])
    mt = mfeat[0]
    for i in range(1, nfeat):
        mt = mt + mfeat[i]
    mtot[core] = mt
    push(mtot.at[core], mtot.at[core], md_s, md_r.at[core], partner, feat)

    for d in range(1, nfeat):
        frm = lax.rem(feat + d, nfeat)
        arrived(sqf.at[frm], sf_s.at[d], sf_r.at[frm])
    sq = sqf[0]
    for i in range(1, nfeat):
        sq = sq + sqf[i]
    sqr[row] = sq
    for d in range(1, nrows):
        push(
            sqr.at[row], sqr.at[row], sr_s.at[d], sr_r.at[row],
            lax.rem(row + d, nrows), feat,
        )

    for d in range(1, chips):
        frm = lax.rem(chip + d, chips)
        arrived(slice_of(frm, core), ag_s.at[d], ag_r.at[frm])
        push(
            slice_of(frm, core), slice_of(frm, core), fw_s.at[d], fw_r.at[frm], partner, feat
        )

    arrived(mtot.at[1 - core], md_s, md_r.at[1 - core])
    grad_models = jnp.concatenate([mtot[0], mtot[1]], axis=0)
    loss_ref[0, 0] = jnp.sum(grad_models[nm:]) / total_rows / float(nfeat)
    grad_models = grad_models[:nm]
    model_square = jnp.sum(grad_models * grad_models)
    for d in range(1, nrows):
        frm = lax.rem(row + d, nrows)
        arrived(sqr.at[frm], sr_s.at[d], sr_r.at[frm])
    sq = sqr[0]
    for i in range(1, nrows):
        sq = sq + sqr[i]
    total = jnp.sum(sq) + model_square
    entries = jnp.sqrt(jnp.full((1, rdim), float(total_dim * rdim + nm * rdim), F32))
    scale = entries / (jnp.sqrt(jnp.full((1, rdim), total, F32)) + 1e-06)
    um_ref[...] = scale * grad_models
    for d in range(chips):
        frm = lax.rem(chip + d, chips)
        arrived(slice_of(frm, 1 - core), fw_s.at[d], fw_r.at[frm])
    out_ref[...] = scale * gfull[...]

    for cp in sent:
        cp.wait_send()
    for to, cp in kept:
        @pl.when(to != chip)
        def _():
            cp.wait_send()


def body(queries, projection, models, first, second, wins):
    nrows, nfeat = lax.axis_size("rows"), lax.axis_size("feat")
    tokens, dloc = queries.shape
    rdim = projection.shape[1]
    nm = models.shape[0]
    chips = nrows // 2
    fs = dloc // nrows
    bw = max(2 * fs, 128)
    blocks = dloc // bw
    half = bw // 2
    gpb = half // fs
    chunks = tokens // 1024
    t = tokens // chunks
    mh = (nm + 16) // 2
    vmem = pl.BlockSpec(memory_space=pltpu.VMEM)
    dma = pltpu.SemaphoreType.DMA
    out, um, loss = pl.pallas_call(
        functools.partial(kernel, nrows, nfeat, chunks, blocks, dloc * nfeat),
        out_shape=(
            jax.ShapeDtypeStruct((dloc, rdim), F32),
            jax.ShapeDtypeStruct((nm, rdim), F32),
            jax.ShapeDtypeStruct((1, 1), F32),
        ),
        in_specs=[pl.BlockSpec(memory_space=pl.ANY)] + [vmem] * 5,
        out_specs=(vmem, vmem, pl.BlockSpec(memory_space=pltpu.SMEM)),
        scratch_shapes=[
            pltpu.VMEM((tokens, dloc), BF16),
            pltpu.VMEM((rdim, tokens), F32),
            pltpu.VMEM((rdim, tokens), F32),
            pltpu.VMEM((rdim, tokens), BF16),
            pltpu.VMEM((nm, tokens), BF16),
            pltpu.VMEM((nfeat, chunks, 1, t), F32),
            pltpu.VMEM((blocks, bw, rdim), F32),
            pltpu.VMEM((blocks, half, rdim), F32),
            pltpu.VMEM((blocks, half, rdim), F32),
            pltpu.VMEM((chips, fs, rdim), F32),
            pltpu.VMEM((dloc, rdim), F32),
            pltpu.VMEM((2 * mh, rdim), F32),
            pltpu.VMEM((mh, rdim), F32),
            pltpu.VMEM((chips, mh, rdim), F32),
            pltpu.VMEM((nfeat, mh, rdim), F32),
            pltpu.VMEM((2, mh, rdim), F32),
            pltpu.VMEM((nfeat, 8, rdim), F32),
            pltpu.VMEM((nrows, 8, rdim), F32),
            dma((chunks,)),
            dma((chunks, nfeat)), dma((chunks, nfeat)),
            dma((blocks,)), dma((blocks,)),
            dma((blocks, gpb)), dma((chips,)),
            dma((chips,)), dma((chips,)),
            dma((chips,)), dma((chips,)),
            dma, dma,
            dma((chips,)), dma((chips,)),
            dma((nfeat,)), dma((nfeat,)),
            dma, dma((2,)),
            dma((nfeat,)), dma((nfeat,)),
            dma((nrows,)), dma((nrows,)),
        ],
        compiler_params=pltpu.CompilerParams(
            collective_id=0, has_side_effects=True, vmem_limit_bytes=60 << 20
        ),
    )(
        queries, projection, models,
        first.reshape(1, tokens), second.reshape(1, tokens), wins.reshape(1, tokens),
    )
    return out, um, loss[0, 0]


def solution(mesh):
    in_specs = (P("rows", "feat"), P("feat", None), P(), P("rows"), P("rows"), P("rows"))
    out_specs = (P("feat", None), P(), P())
    return jax.shard_map(body, mesh=mesh, in_specs=in_specs, out_specs=out_specs, check_vma=False)
```

```python
import functools

import jax
import jax.numpy as jnp
from jax import lax
from jax.experimental import pallas as pl
from jax.experimental.pallas import tpu as pltpu
from jax.sharding import PartitionSpec as P

F32 = jnp.float32
BF16 = jnp.bfloat16
SUB = 256
MESH = pl.DeviceIdType.MESH
NT = (((1,), (1,)), ((), ()))


def dot_nt(a, b):
    return lax.dot_general(a, b, NT, preferred_element_type=F32)


def split3(x):
    hi = x.astype(BF16)
    rest = x - hi.astype(F32)
    mid = rest.astype(BF16)
    lo = (rest - mid.astype(F32)).astype(BF16)
    return hi, mid, lo


def kernel(
    nrows, nfeat, chunks, blocks, total_dim,
    q_hbm, proj_hbm, models_hbm, first_hbm, second_hbm, wins_hbm,
    out_ref, small_ref,
    qv, proj_ref, models_ref, first_ref, second_ref, wins_ref,
    gap_v, routed_v, back_v, pick_v, marg, acc_v, gblk, prt, csum, rbuf, gfull,
    mbuf, mprt, mrow, mfeat, mtot, sqf, sqr,
    q_sem, in_sem, mg_s, mg_r, pr_s, pr_r, rs_s, rs_r, ag_s, ag_r, fw_s, fw_r,
    ma_s, ma_r, mb_s, mb_r, mc_s, mc_r, md_s, md_r, sf_s, sf_r, sr_s, sr_r,
):
    row = lax.axis_index("rows")
    feat = lax.axis_index("feat")
    core = lax.rem(row, 2)
    chip = lax.div(row, 2)
    chips = nrows // 2
    partner = chip * 2 + (1 - core)
    tokens, dloc = qv.shape
    rdim = proj_ref.shape[1]
    nm = models_ref.shape[0]
    t = tokens // chunks
    early = max(1, chunks * 2 // 3)
    bw = dloc // blocks
    half = bw // 2
    fs = dloc // nrows
    gpb = half // fs
    mh = mbuf.shape[0] // 2
    total_rows = float(tokens * nrows)

    def qcopy(c):
        at = pl.ds(c * t, t)
        return pltpu.make_async_copy(q_hbm.at[at], qv.at[at], q_sem.at[c])

    small_inputs = [
        pltpu.make_async_copy(src, dst, in_sem.at[n])
        for n, (src, dst) in enumerate((
            (models_hbm, models_ref), (first_hbm, first_ref), (second_hbm, second_ref),
            (proj_hbm, proj_ref), (wins_hbm, wins_ref),
        ))
    ]
    for cp in small_inputs:
        cp.start()
    for c in range(chunks):
        qcopy(c).start()

    barrier = pltpu.get_barrier_semaphore()
    for d in range(1, nfeat):
        pl.semaphore_signal(
            barrier, inc=1, device_id=(row, lax.rem(feat + d, nfeat)), device_id_type=MESH
        )
    for d in range(1, nrows):
        pl.semaphore_signal(
            barrier, inc=1, device_id=(lax.rem(row + d, nrows), feat), device_id_type=MESH
        )

    def other(d):
        if chips != 4:
            return lax.rem(chip + d, chips)
        y, x = lax.div(chip, 2), lax.rem(chip, 2)
        return ((y * 2 + 1 - x), ((1 - y) * 2 + x), ((1 - y) * 2 + 1 - x))[d - 1]

    def remote(src, dst, send, recv, to_row, to_feat):
        return pltpu.make_async_remote_copy(
            src_ref=src, dst_ref=dst, send_sem=send, recv_sem=recv,
            device_id=(to_row, to_feat), device_id_type=MESH,
        )

    def push(*args):
        remote(*args).start()

    def arrived(view, recv):
        remote(view, view, recv, recv, partner, feat).wait_recv()

    def all_sent(view, send):
        remote(view, view, send, send, partner, feat).wait_send()

    eye = (
        lax.broadcasted_iota(jnp.int32, (rdim, rdim), 0)
        == lax.broadcasted_iota(jnp.int32, (rdim, rdim), 1)
    ).astype(F32).astype(BF16)
    for cp in small_inputs[:3]:
        cp.wait()
    models3 = jnp.concatenate(split3(models_ref[...]), axis=0)
    models3_t = dot_nt(eye, models3).astype(BF16)

    label = lax.broadcasted_iota(jnp.int32, (nm, SUB), 0)
    for s in range(tokens // SUB):
        at = pl.ds(s * SUB, SUB)
        pick = (
            (label == first_ref[:, at]).astype(F32) - (label == second_ref[:, at]).astype(F32)
        ).astype(BF16)
        pick_v[:, at] = pick
        pick3 = jnp.concatenate([pick, pick, pick], axis=0)
        gap_v[:, at] = jnp.dot(models3_t, pick3, preferred_element_type=F32)

    for cp in small_inputs[3:]:
        cp.wait()
    proj_t = dot_nt(eye, proj_ref[...]).astype(BF16)

    def partial_margins(c):
        qcopy(c).wait()
        for s in range(t // SUB):
            at = pl.ds(c * t + s * SUB, SUB)
            routed = dot_nt(proj_t, qv[at, :])
            routed_v[:, at] = routed
            marg[feat, :, at] = jnp.sum(routed * gap_v[:, at], axis=0, keepdims=True)

    groups = (range(early), range(early, chunks))

    def cut(g):
        return pl.ds(groups[g].start * t, len(groups[g]) * t)

    for g in range(2):
        for c in groups[g]:
            partial_margins(c)
        if g == 0:
            pl.semaphore_wait(barrier, nfeat - 1 + nrows - 1)
        for d in range(1, nfeat):
            view = marg.at[feat, :, cut(g)]
            push(view, view, mg_s, mg_r.at[g], row, lax.rem(feat + d, nfeat))

    def block_of(i):
        if gpb == 1 and chips == 4:
            return other(3 - i) if i < 3 else chip
        return lax.rem(lax.div(chip, gpb) + 1 + i, blocks)

    def block_part(i, g, acc):
        cols = pl.ds(pl.multiple_of(block_of(i) * bw, 128), bw)
        for c in groups[g]:
            at = pl.ds(c * t, t)
            acc = acc + jnp.dot(back_v[:, at], qv[at, cols], preferred_element_type=F32)
        return acc

    loss_row = jnp.zeros((1, t), F32)
    msum = jnp.zeros((nm, 2 * rdim), F32)
    for g in range(2):
        arrived(marg.at[pl.ds(0, nfeat - 1), :, cut(g)], mg_r.at[g])
        for c in groups[g]:
            at = pl.ds(c * t, t)
            margin = marg[0, :, at]
            for z in range(1, nfeat):
                margin = margin + marg[z, :, at]
            sign = 2.0 * wins_ref[:, at].astype(F32) - 1.0
            x = -sign * margin
            loss_row = loss_row + (jnp.maximum(x, 0.0) + jnp.log1p(jnp.exp(-jnp.abs(x))))
            coef = -sign * jax.nn.sigmoid(x) / total_rows
            for s in range(t // SUB):
                sub = pl.ds(c * t + s * SUB, SUB)
                cs = coef[:, s * SUB:(s + 1) * SUB]
                back_v[:, sub] = (cs * gap_v[:, sub]).astype(BF16)
                w = cs * routed_v[:, sub]
                hi = w.astype(BF16)
                lo = (w - hi.astype(F32)).astype(BF16)
                msum = msum + dot_nt(pick_v[:, sub], jnp.concatenate([hi, lo], axis=0))
        if g == 0:
            for i in range(blocks):
                acc_v[i] = block_part(i, 0, jnp.zeros((rdim, bw), F32))

    mbuf[0:nm, :] = msum[:, :rdim] + msum[:, rdim:]
    lsum = loss_row[:, 0:rdim]
    for i in range(1, t // rdim):
        lsum = lsum + loss_row[:, i * rdim:(i + 1) * rdim]
    tail = mbuf.shape[0] - nm
    mbuf[nm:, :] = jnp.where(
        lax.broadcasted_iota(jnp.int32, (tail, rdim), 0) == 0,
        jnp.broadcast_to(lsum, (tail, rdim)), 0.0,
    )
    push(mbuf.at[pl.ds((1 - core) * mh, mh)], mprt, ma_s, ma_r, partner, feat)

    def block_grad(i):
        gblk[i] = block_part(i, 1, acc_v[i]).T
        push(gblk.at[i, pl.ds((1 - core) * half, half)], prt.at[i], pr_s, pr_r.at[i], partner, feat)

    def chip_sum(i):
        arrived(prt.at[i], pr_r.at[i])
        csum[i] = gblk[i, pl.ds(core * half, half), :] + prt[i]
        for j in range(gpb):
            to = block_of(i) * gpb + j
            mine = pl.ds(j * fs, fs)

            def send():
                push(csum.at[i, mine], rbuf.at[chip], rs_s, rs_r, to * 2 + core, feat)

            def keep():
                rbuf[chip] = csum[i, mine, :]

            if gpb > 1:
                pl.when(to != chip)(send)
                pl.when(to == chip)(keep)
            elif i < blocks - 1:
                send()
            else:
                keep()

    for i in range(blocks):
        block_grad(i)
        if i > 0:
            chip_sum(i - 1)
    arrived(mprt, ma_r)
    mrow[chip] = mbuf[pl.ds(core * mh, mh), :] + mprt[...]
    for d in range(chips - 1, 0, -1):
        push(mrow.at[chip], mrow.at[chip], mb_s, mb_r, other(d) * 2 + core, feat)
    chip_sum(blocks - 1)
    arrived(mrow.at[pl.ds(0, chips - 1)], mb_r)
    mr = mrow[0]
    for i in range(1, chips):
        mr = mr + mrow[i]
    mfeat[feat] = mr
    for d in range(1, nfeat):
        push(mfeat.at[feat], mfeat.at[feat], mc_s, mc_r, row, lax.rem(feat + d, nfeat))

    def slice_of(c, k):
        start = lax.div(c, gpb) * bw + k * half + lax.rem(c, gpb) * fs
        return gfull.at[pl.ds(pl.multiple_of(start, 8), fs)]

    arrived(rbuf.at[pl.ds(0, chips - 1)], rs_r)
    own = rbuf[0]
    for i in range(1, chips):
        own = own + rbuf[i]
    mine = slice_of(chip, core)
    mine[...] = own
    for d in range(chips - 1, 0, -1):
        push(mine, mine, ag_s, ag_r.at[chip], other(d) * 2 + core, feat)
    push(mine, mine, fw_s, fw_r, partner, feat)
    square = own * own
    sq = square[0:8]
    for i in range(1, fs // 8):
        sq = sq + square[i * 8:(i + 1) * 8]
    sqf[feat] = sq
    for d in range(1, nfeat):
        push(sqf.at[feat], sqf.at[feat], sf_s, sf_r, row, lax.rem(feat + d, nfeat))

    arrived(sqf.at[pl.ds(0, nfeat - 1)], sf_r)
    sq = sqf[0]
    for i in range(1, nfeat):
        sq = sq + sqf[i]
    sqr[row] = sq
    for d in range(1, nrows):
        push(sqr.at[row], sqr.at[row], sr_s, sr_r, lax.rem(row + d, nrows), feat)

    arrived(mfeat.at[pl.ds(0, nfeat - 1)], mc_r)
    mt = mfeat[0]
    for i in range(1, nfeat):
        mt = mt + mfeat[i]
    mtot[core] = mt
    push(mtot.at[core], mtot.at[core], md_s, md_r, partner, feat)

    for d in range(1, chips):
        view = slice_of(other(d), core)
        arrived(view, ag_r.at[other(d)])
        push(view, view, fw_s, fw_r, partner, feat)

    all_sent(marg.at[pl.ds(0, nfeat - 1)], mg_s)
    all_sent(mprt, ma_s)
    all_sent(mrow.at[pl.ds(0, chips - 1)], mb_s)
    all_sent(mfeat.at[pl.ds(0, nfeat - 1)], mc_s)
    all_sent(prt, pr_s)
    all_sent(rbuf.at[pl.ds(0, chips - 1)], rs_s)
    all_sent(rbuf.at[pl.ds(0, chips - 1)], ag_s)
    all_sent(sqf.at[pl.ds(0, nfeat - 1)], sf_s)

    arrived(mtot.at[1 - core], md_r)
    grad_models = jnp.concatenate([mtot[0], mtot[1]], axis=0)
    loss = jnp.sum(grad_models[nm:]) / total_rows / float(nfeat)
    grad_models = grad_models[:nm]
    model_square = jnp.sum(grad_models * grad_models)
    small_ref[0:nm] = grad_models
    small_ref[nm + 8:] = jnp.full((8, rdim), loss, F32)
    arrived(sqr.at[pl.ds(0, nrows - 1)], sr_r)
    sq = sqr[0]
    for i in range(1, nrows):
        sq = sq + sqr[i]
    total = jnp.sum(sq) + model_square
    entries = jnp.sqrt(jnp.full((8, rdim), float(total_dim * rdim + nm * rdim), F32))
    small_ref[nm:nm + 8] = entries / (jnp.sqrt(jnp.full((8, rdim), total, F32)) + 1e-06)
    arrived(prt, fw_r)
    out_ref[...] = gfull[...]
    all_sent(mtot.at[0], md_s)
    all_sent(sqr.at[pl.ds(0, nrows - 1)], sr_s)
    all_sent(prt, fw_s)


def finish(nm, grad_ref, small_ref, out_ref, um_ref, loss_ref):
    scale = small_ref[nm:nm + 1, :]
    out_ref[...] = scale * grad_ref[...]
    um_ref[...] = scale * small_ref[0:nm, :]
    loss_ref[0, 0] = small_ref[nm + 8, 0]


def body(queries, projection, models, first, second, wins):
    nrows, nfeat = lax.axis_size("rows"), lax.axis_size("feat")
    tokens, dloc = queries.shape
    rdim = projection.shape[1]
    nm = models.shape[0]
    chips = nrows // 2
    fs = dloc // nrows
    bw = max(2 * fs, 128)
    blocks = dloc // bw
    half = bw // 2
    chunks = tokens // 1024
    mh = (nm + 16) // 2
    vmem = pl.BlockSpec(memory_space=pltpu.VMEM)
    hbm = pl.BlockSpec(memory_space=pl.ANY)
    dma = pltpu.SemaphoreType.DMA
    grad, small = pl.pallas_call(
        functools.partial(kernel, nrows, nfeat, chunks, blocks, dloc * nfeat),
        out_shape=(
            jax.ShapeDtypeStruct((dloc, rdim), F32),
            jax.ShapeDtypeStruct((nm + 16, rdim), F32),
        ),
        in_specs=[hbm] * 6,
        out_specs=(vmem, vmem),
        scratch_shapes=[
            pltpu.VMEM((tokens, dloc), BF16),
            pltpu.VMEM((dloc, rdim), BF16),
            pltpu.VMEM((nm, rdim), F32),
            pltpu.VMEM((1, tokens), jnp.int32),
            pltpu.VMEM((1, tokens), jnp.int32),
            pltpu.VMEM((1, tokens), jnp.int32),
            pltpu.VMEM((rdim, tokens), F32),
            pltpu.VMEM((rdim, tokens), F32),
            pltpu.VMEM((rdim, tokens), BF16),
            pltpu.VMEM((nm, tokens), BF16),
            pltpu.VMEM((nfeat, 1, tokens), F32),
            pltpu.VMEM((blocks, rdim, bw), F32),
            pltpu.VMEM((blocks, bw, rdim), F32),
            pltpu.VMEM((blocks, half, rdim), F32),
            pltpu.VMEM((blocks, half, rdim), F32),
            pltpu.VMEM((chips, fs, rdim), F32),
            pltpu.VMEM((dloc, rdim), F32),
            pltpu.VMEM((2 * mh, rdim), F32),
            pltpu.VMEM((mh, rdim), F32),
            pltpu.VMEM((chips, mh, rdim), F32),
            pltpu.VMEM((nfeat, mh, rdim), F32),
            pltpu.VMEM((2, mh, rdim), F32),
            pltpu.VMEM((nfeat, 8, rdim), F32),
            pltpu.VMEM((nrows, 8, rdim), F32),
            dma((chunks,)), dma((5,)),
            dma, dma((2,)),
            dma, dma((blocks,)),
            dma, dma,
            dma, dma((chips,)),
            dma, dma,
            dma, dma,
            dma, dma,
            dma, dma,
            dma, dma,
            dma, dma,
            dma, dma,
        ],
        compiler_params=pltpu.CompilerParams(
            collective_id=0, has_side_effects=True, vmem_limit_bytes=60 << 20
        ),
    )(
        queries, projection, models,
        first.reshape(1, tokens), second.reshape(1, tokens), wins.reshape(1, tokens),
    )
    out, um, loss = pl.pallas_call(
        functools.partial(finish, nm),
        out_shape=(
            jax.ShapeDtypeStruct((dloc, rdim), F32),
            jax.ShapeDtypeStruct((nm, rdim), F32),
            jax.ShapeDtypeStruct((1, 1), F32),
        ),
        in_specs=[vmem, vmem],
        out_specs=(vmem, vmem, pl.BlockSpec(memory_space=pltpu.SMEM)),
        name="finish",
    )(grad, small)
    return out, um, loss[0, 0]


def solution(mesh):
    in_specs = (P("rows", "feat"), P("feat", None), P(), P("rows"), P("rows"), P("rows"))
    out_specs = (P("feat", None), P(), P())
    return jax.shard_map(body, mesh=mesh, in_specs=in_specs, out_specs=out_specs, check_vma=False)
```

```python
import functools

import jax
import jax.numpy as jnp
from jax import lax
from jax.experimental import pallas as pl
from jax.experimental.pallas import tpu as pltpu
from jax.sharding import PartitionSpec as P

F32 = jnp.float32
BF16 = jnp.bfloat16
SUB = 256
MESH = pl.DeviceIdType.MESH
NT = (((1,), (1,)), ((), ()))


def dot_nt(a, b):
    return lax.dot_general(a, b, NT, preferred_element_type=F32)


def split3(x):
    hi = x.astype(BF16)
    rest = x - hi.astype(F32)
    mid = rest.astype(BF16)
    lo = (rest - mid.astype(F32)).astype(BF16)
    return hi, mid, lo


def kernel(
    nrows, nfeat, chunks, blocks, total_dim,
    q_hbm, proj_hbm, models_hbm, first_hbm, second_hbm, wins_hbm,
    out_ref, small_ref,
    qv, proj_ref, models_ref, first_ref, second_ref, wins_ref,
    gap_v, routed_v, back_v, pick_v, marg, acc_v, gblk, prt, csum, rbuf, gfull,
    mbuf, mprt, mrow, mfeat, mtot, sqf, sqr,
    q_sem, in_sem, mg_s, mg_r, pr_s, pr_r, rs_s, rs_r, ag_s, ag_r, fw_s, fw_r,
    ma_s, ma_r, mb_s, mb_r, mc_s, mc_r, md_s, md_r, sf_s, sf_r, sr_s, sr_r,
):
    row = lax.axis_index("rows")
    feat = lax.axis_index("feat")
    core = lax.rem(row, 2)
    chip = lax.div(row, 2)
    chips = nrows // 2
    partner = chip * 2 + (1 - core)
    tokens, dloc = qv.shape
    rdim = proj_ref.shape[1]
    nm = models_ref.shape[0]
    t = tokens // chunks
    ngroups = mg_r.shape[0]
    bw = dloc // blocks
    half = bw // 2
    fs = dloc // nrows
    gpb = half // fs
    mh = mbuf.shape[0] // 2
    total_rows = float(tokens * nrows)

    pieces = q_sem.shape[0]
    flight = 5
    piece = tokens // pieces
    state = {"started": 0, "ready": 0}

    def qcopy(n):
        at = pl.ds(n * piece, piece)
        return pltpu.make_async_copy(q_hbm.at[at], qv.at[at], q_sem.at[n])

    def stream_to(count):
        while state["started"] < min(count, pieces):
            qcopy(state["started"]).start()
            state["started"] += 1

    def ready_to(count):
        while state["ready"] < min(count, pieces):
            qcopy(state["ready"]).wait()
            state["ready"] += 1
            stream_to(state["ready"] + flight)

    small_inputs = [
        pltpu.make_async_copy(src, dst, in_sem.at[n])
        for n, (src, dst) in enumerate((
            (models_hbm, models_ref), (first_hbm, first_ref), (second_hbm, second_ref),
            (proj_hbm, proj_ref), (wins_hbm, wins_ref),
        ))
    ]
    for cp in small_inputs:
        cp.start()
    stream_to(flight)

    barrier = pltpu.get_barrier_semaphore()
    for d in range(1, nfeat):
        pl.semaphore_signal(
            barrier, inc=1, device_id=(row, lax.rem(feat + d, nfeat)), device_id_type=MESH
        )
    for d in range(1, nrows):
        pl.semaphore_signal(
            barrier, inc=1, device_id=(lax.rem(row + d, nrows), feat), device_id_type=MESH
        )

    def other(d):
        if chips != 4:
            return lax.rem(chip + d, chips)
        y, x = lax.div(chip, 2), lax.rem(chip, 2)
        return ((y * 2 + 1 - x), ((1 - y) * 2 + x), ((1 - y) * 2 + 1 - x))[d - 1]

    def remote(src, dst, send, recv, to_row, to_feat):
        return pltpu.make_async_remote_copy(
            src_ref=src, dst_ref=dst, send_sem=send, recv_sem=recv,
            device_id=(to_row, to_feat), device_id_type=MESH,
        )

    def push(*args):
        remote(*args).start()

    def arrived(view, recv):
        remote(view, view, recv, recv, partner, feat).wait_recv()

    def all_sent(view, send):
        remote(view, view, send, send, partner, feat).wait_send()

    eye = (
        lax.broadcasted_iota(jnp.int32, (rdim, rdim), 0)
        == lax.broadcasted_iota(jnp.int32, (rdim, rdim), 1)
    ).astype(F32).astype(BF16)
    for cp in small_inputs[:3]:
        cp.wait()
    models3 = jnp.concatenate(split3(models_ref[...]), axis=0)
    models3_t = dot_nt(eye, models3).astype(BF16)

    label = lax.broadcasted_iota(jnp.int32, (nm, SUB), 0)
    for s in range(tokens // SUB):
        at = pl.ds(s * SUB, SUB)
        pick = (
            (label == first_ref[:, at]).astype(F32) - (label == second_ref[:, at]).astype(F32)
        ).astype(BF16)
        pick_v[:, at] = pick
        pick3 = jnp.concatenate([pick, pick, pick], axis=0)
        gap_v[:, at] = jnp.dot(models3_t, pick3, preferred_element_type=F32)
        if s % 6 == 5:
            ready_to(min(s // 6 + 1, 3))

    for cp in small_inputs[3:]:
        cp.wait()
    proj_t = dot_nt(eye, proj_ref[...]).astype(BF16)

    def partial_margins(c):
        for s in range(t // SUB):
            ready_to(((c * t + (s + 1) * SUB - 1) // piece) + 1)
            at = pl.ds(c * t + s * SUB, SUB)
            routed = dot_nt(proj_t, qv[at, :])
            routed_v[:, at] = routed
            marg[feat, :, at] = jnp.sum(routed * gap_v[:, at], axis=0, keepdims=True)

    ends = [chunks * (g + 1) // ngroups for g in range(ngroups)]
    groups = [range(a, b) for a, b in zip([0] + ends[:-1], ends)]

    def cut(g):
        return pl.ds(groups[g].start * t, len(groups[g]) * t)

    for g in range(ngroups):
        for c in groups[g]:
            partial_margins(c)
        if g == 0:
            pl.semaphore_wait(barrier, nfeat - 1 + nrows - 1)
        for d in range(1, nfeat):
            view = marg.at[feat, :, cut(g)]
            push(view, view, mg_s, mg_r.at[g], row, lax.rem(feat + d, nfeat))

    def block_of(i):
        if gpb == 1 and chips == 4:
            return other(3 - i) if i < 3 else chip
        return lax.rem(lax.div(chip, gpb) + 1 + i, blocks)

    def block_part(i, g, acc):
        cols = pl.ds(pl.multiple_of(block_of(i) * bw, 128), bw)
        for c in groups[g]:
            at = pl.ds(c * t, t)
            acc = acc + jnp.dot(back_v[:, at], qv[at, cols], preferred_element_type=F32)
        return acc

    loss_row = jnp.zeros((1, t), F32)
    msum = jnp.zeros((nm, 2 * rdim), F32)
    for g in range(ngroups):
        arrived(marg.at[pl.ds(0, nfeat - 1), :, cut(g)], mg_r.at[g])
        for c in groups[g]:
            at = pl.ds(c * t, t)
            margin = marg[0, :, at]
            for z in range(1, nfeat):
                margin = margin + marg[z, :, at]
            sign = 2.0 * wins_ref[:, at].astype(F32) - 1.0
            x = -sign * margin
            loss_row = loss_row + (jnp.maximum(x, 0.0) + jnp.log1p(jnp.exp(-jnp.abs(x))))
            coef = -sign * jax.nn.sigmoid(x) / total_rows
            for s in range(t // SUB):
                sub = pl.ds(c * t + s * SUB, SUB)
                cs = coef[:, s * SUB:(s + 1) * SUB]
                back_v[:, sub] = (cs * gap_v[:, sub]).astype(BF16)
                w = cs * routed_v[:, sub]
                hi = w.astype(BF16)
                lo = (w - hi.astype(F32)).astype(BF16)
                msum = msum + dot_nt(pick_v[:, sub], jnp.concatenate([hi, lo], axis=0))
        if g < ngroups - 1:
            for i in range(blocks):
                acc = jnp.zeros((rdim, bw), F32) if g == 0 else acc_v[i]
                acc_v[i] = block_part(i, g, acc)

    mbuf[0:nm, :] = msum[:, :rdim] + msum[:, rdim:]
    lsum = loss_row[:, 0:rdim]
    for i in range(1, t // rdim):
        lsum = lsum + loss_row[:, i * rdim:(i + 1) * rdim]
    tail = mbuf.shape[0] - nm
    mbuf[nm:, :] = jnp.where(
        lax.broadcasted_iota(jnp.int32, (tail, rdim), 0) == 0,
        jnp.broadcast_to(lsum, (tail, rdim)), 0.0,
    )
    push(mbuf.at[pl.ds((1 - core) * mh, mh)], mprt, ma_s, ma_r, partner, feat)

    def block_grad(i):
        gblk[i] = block_part(i, ngroups - 1, acc_v[i]).T
        push(gblk.at[i, pl.ds((1 - core) * half, half)], prt.at[i], pr_s, pr_r.at[i], partner, feat)

    def chip_sum(i):
        arrived(prt.at[i], pr_r.at[i])
        csum[i] = gblk[i, pl.ds(core * half, half), :] + prt[i]
        for j in range(gpb):
            to = block_of(i) * gpb + j
            mine = pl.ds(j * fs, fs)

            def send():
                push(csum.at[i, mine], rbuf.at[chip], rs_s, rs_r, to * 2 + core, feat)

            def keep():
                rbuf[chip] = csum[i, mine, :]

            if gpb > 1:
                pl.when(to != chip)(send)
                pl.when(to == chip)(keep)
            elif i < blocks - 1:
                send()
            else:
                keep()

    def models_chip():
        arrived(mprt, ma_r)
        mrow[chip] = mbuf[pl.ds(core * mh, mh), :] + mprt[...]
        for d in range(chips - 1, 0, -1):
            push(mrow.at[chip], mrow.at[chip], mb_s, mb_r, other(d) * 2 + core, feat)

    for i in range(blocks):
        block_grad(i)
        if i == min(2, blocks - 1):
            models_chip()
        if i >= 2:
            chip_sum(i - 2)
    chip_sum(blocks - 2)
    chip_sum(blocks - 1)
    arrived(mrow.at[pl.ds(0, chips - 1)], mb_r)
    mr = mrow[0]
    for i in range(1, chips):
        mr = mr + mrow[i]
    mfeat[feat] = mr
    for d in range(1, nfeat):
        push(mfeat.at[feat], mfeat.at[feat], mc_s, mc_r, row, lax.rem(feat + d, nfeat))

    def slice_of(c, k):
        start = lax.div(c, gpb) * bw + k * half + lax.rem(c, gpb) * fs
        return gfull.at[pl.ds(pl.multiple_of(start, 8), fs)]

    arrived(rbuf.at[pl.ds(0, chips - 1)], rs_r)
    own = rbuf[0]
    for i in range(1, chips):
        own = own + rbuf[i]
    mine = slice_of(chip, core)
    mine[...] = own
    for d in range(chips - 1, 0, -1):
        push(mine, mine, ag_s, ag_r.at[chip], other(d) * 2 + core, feat)
    push(mine, mine, fw_s, fw_r, partner, feat)
    square = own * own
    sq = square[0:8]
    for i in range(1, fs // 8):
        sq = sq + square[i * 8:(i + 1) * 8]
    sqf[feat] = sq
    for d in range(1, nfeat):
        push(sqf.at[feat], sqf.at[feat], sf_s, sf_r, row, lax.rem(feat + d, nfeat))

    arrived(sqf.at[pl.ds(0, nfeat - 1)], sf_r)
    sq = sqf[0]
    for i in range(1, nfeat):
        sq = sq + sqf[i]
    sqr[row] = sq
    for d in range(1, nrows):
        push(sqr.at[row], sqr.at[row], sr_s, sr_r, lax.rem(row + d, nrows), feat)

    arrived(mfeat.at[pl.ds(0, nfeat - 1)], mc_r)
    mt = mfeat[0]
    for i in range(1, nfeat):
        mt = mt + mfeat[i]
    mtot[core] = mt
    push(mtot.at[core], mtot.at[core], md_s, md_r, partner, feat)

    for d in range(1, chips):
        view = slice_of(other(d), core)
        arrived(view, ag_r.at[other(d)])
        push(view, view, fw_s, fw_r, partner, feat)

    all_sent(marg.at[pl.ds(0, nfeat - 1)], mg_s)
    all_sent(mprt, ma_s)
    all_sent(mrow.at[pl.ds(0, chips - 1)], mb_s)
    all_sent(mfeat.at[pl.ds(0, nfeat - 1)], mc_s)
    all_sent(prt, pr_s)
    all_sent(rbuf.at[pl.ds(0, chips - 1)], rs_s)
    all_sent(rbuf.at[pl.ds(0, chips - 1)], ag_s)
    all_sent(sqf.at[pl.ds(0, nfeat - 1)], sf_s)

    arrived(mtot.at[1 - core], md_r)
    grad_models = jnp.concatenate([mtot[0], mtot[1]], axis=0)
    loss = jnp.sum(grad_models[nm:]) / total_rows / float(nfeat)
    grad_models = grad_models[:nm]
    model_square = jnp.sum(grad_models * grad_models)
    small_ref[0:nm] = grad_models
    small_ref[nm + 8:] = jnp.full((8, rdim), loss, F32)
    arrived(sqr.at[pl.ds(0, nrows - 1)], sr_r)
    sq = sqr[0]
    for i in range(1, nrows):
        sq = sq + sqr[i]
    total = jnp.sum(sq) + model_square
    entries = jnp.sqrt(jnp.full((8, rdim), float(total_dim * rdim + nm * rdim), F32))
    small_ref[nm:nm + 8] = entries / (jnp.sqrt(jnp.full((8, rdim), total, F32)) + 1e-06)
    arrived(prt, fw_r)
    out_ref[...] = gfull[...]
    all_sent(mtot.at[0], md_s)
    all_sent(sqr.at[pl.ds(0, nrows - 1)], sr_s)
    all_sent(prt, fw_s)


def finish(nm, grad_ref, small_ref, out_ref, um_ref, loss_ref):
    scale = small_ref[nm:nm + 1, :]
    out_ref[...] = scale * grad_ref[...]
    um_ref[...] = scale * small_ref[0:nm, :]
    loss_ref[0, 0] = small_ref[nm + 8, 0]


def body(queries, projection, models, first, second, wins):
    nrows, nfeat = lax.axis_size("rows"), lax.axis_size("feat")
    tokens, dloc = queries.shape
    rdim = projection.shape[1]
    nm = models.shape[0]
    chips = nrows // 2
    fs = dloc // nrows
    bw = max(2 * fs, 128)
    blocks = dloc // bw
    half = bw // 2
    chunks = tokens // 1024
    mh = (nm + 16) // 2
    vmem = pl.BlockSpec(memory_space=pltpu.VMEM)
    hbm = pl.BlockSpec(memory_space=pl.ANY)
    dma = pltpu.SemaphoreType.DMA
    grad, small = pl.pallas_call(
        functools.partial(kernel, nrows, nfeat, chunks, blocks, dloc * nfeat),
        out_shape=(
            jax.ShapeDtypeStruct((dloc, rdim), F32),
            jax.ShapeDtypeStruct((nm + 16, rdim), F32),
        ),
        in_specs=[hbm] * 6,
        out_specs=(vmem, vmem),
        scratch_shapes=[
            pltpu.VMEM((tokens, dloc), BF16),
            pltpu.VMEM((dloc, rdim), BF16),
            pltpu.VMEM((nm, rdim), F32),
            pltpu.VMEM((1, tokens), jnp.int32),
            pltpu.VMEM((1, tokens), jnp.int32),
            pltpu.VMEM((1, tokens), jnp.int32),
            pltpu.VMEM((rdim, tokens), F32),
            pltpu.VMEM((rdim, tokens), F32),
            pltpu.VMEM((rdim, tokens), BF16),
            pltpu.VMEM((nm, tokens), BF16),
            pltpu.VMEM((nfeat, 1, tokens), F32),
            pltpu.VMEM((blocks, rdim, bw), F32),
            pltpu.VMEM((blocks, bw, rdim), F32),
            pltpu.VMEM((blocks, half, rdim), F32),
            pltpu.VMEM((blocks, half, rdim), F32),
            pltpu.VMEM((chips, fs, rdim), F32),
            pltpu.VMEM((dloc, rdim), F32),
            pltpu.VMEM((2 * mh, rdim), F32),
            pltpu.VMEM((mh, rdim), F32),
            pltpu.VMEM((chips, mh, rdim), F32),
            pltpu.VMEM((nfeat, mh, rdim), F32),
            pltpu.VMEM((2, mh, rdim), F32),
            pltpu.VMEM((nfeat, 8, rdim), F32),
            pltpu.VMEM((nrows, 8, rdim), F32),
            dma((tokens // 512,)), dma((5,)),
            dma, dma((3,)),
            dma, dma((blocks,)),
            dma, dma,
            dma, dma((chips,)),
            dma, dma,
            dma, dma,
            dma, dma,
            dma, dma,
            dma, dma,
            dma, dma,
            dma, dma,
        ],
        compiler_params=pltpu.CompilerParams(
            collective_id=0, has_side_effects=True, vmem_limit_bytes=60 << 20
        ),
    )(
        queries, projection, models,
        first.reshape(1, tokens), second.reshape(1, tokens), wins.reshape(1, tokens),
    )
    out, um, loss = pl.pallas_call(
        functools.partial(finish, nm),
        out_shape=(
            jax.ShapeDtypeStruct((dloc, rdim), F32),
            jax.ShapeDtypeStruct((nm, rdim), F32),
            jax.ShapeDtypeStruct((1, 1), F32),
        ),
        in_specs=[vmem, vmem],
        out_specs=(vmem, vmem, pl.BlockSpec(memory_space=pltpu.SMEM)),
        name="finish",
    )(grad, small)
    return out, um, loss[0, 0]


def solution(mesh):
    in_specs = (P("rows", "feat"), P("feat", None), P(), P("rows"), P("rows"), P("rows"))
    out_specs = (P("feat", None), P(), P())
    return jax.shard_map(body, mesh=mesh, in_specs=in_specs, out_specs=out_specs, check_vma=False)
```

```python
import functools

import jax
import jax.numpy as jnp
from jax import lax
from jax.experimental import pallas as pl
from jax.experimental.pallas import tpu as pltpu
from jax.sharding import PartitionSpec as P

F32 = jnp.float32
BF16 = jnp.bfloat16
SUB = 256
MESH = pl.DeviceIdType.MESH
NT = (((1,), (1,)), ((), ()))


def dot_nt(a, b):
    return lax.dot_general(a, b, NT, preferred_element_type=F32)


def split3(x):
    hi = x.astype(BF16)
    rest = x - hi.astype(F32)
    mid = rest.astype(BF16)
    lo = (rest - mid.astype(F32)).astype(BF16)
    return hi, mid, lo


def kernel(
    nrows, nfeat, chunks, blocks, total_dim,
    q_hbm, proj_hbm, models_hbm, first_hbm, second_hbm, wins_hbm,
    out_ref, small_ref,
    qv, proj_ref, models_ref, first_ref, second_ref, wins_ref,
    gap_v, routed_v, back_v, pick_v, marg, acc_v, gblk, prt, csum, rbuf, gfull,
    mbuf, mprt, mrow, mfeat, mtot, sqf, sqr,
    q_sem, in_sem, mg_s, mg_r, pr_s, pr_r, rs_s, rs_r, ag_s, ag_r, fw_s, fw_r,
    ma_s, ma_r, mb_s, mb_r, mc_s, mc_r, md_s, md_r, sf_s, sf_r, sr_s, sr_r,
):
    row = lax.axis_index("rows")
    feat = lax.axis_index("feat")
    core = lax.rem(row, 2)
    chip = lax.div(row, 2)
    chips = nrows // 2
    partner = chip * 2 + (1 - core)
    tokens, dloc = qv.shape
    rdim = proj_ref.shape[1]
    nm = models_ref.shape[0]
    t = tokens // chunks
    ngroups = mg_r.shape[0]
    bw = dloc // blocks
    half = bw // 2
    fs = dloc // nrows
    gpb = half // fs
    mh = mbuf.shape[0] // 2
    total_rows = float(tokens * nrows)

    pieces = q_sem.shape[0]
    flight = 5
    piece = tokens // pieces
    state = {"started": 0, "ready": 0}

    def qcopy(n):
        at = pl.ds(n * piece, piece)
        return pltpu.make_async_copy(q_hbm.at[at], qv.at[at], q_sem.at[n])

    def stream_to(count):
        while state["started"] < min(count, pieces):
            qcopy(state["started"]).start()
            state["started"] += 1

    def ready_to(count):
        while state["ready"] < min(count, pieces):
            qcopy(state["ready"]).wait()
            state["ready"] += 1
            stream_to(state["ready"] + flight)

    small_inputs = [
        pltpu.make_async_copy(src, dst, in_sem.at[n])
        for n, (src, dst) in enumerate((
            (models_hbm, models_ref), (first_hbm, first_ref), (second_hbm, second_ref),
            (proj_hbm, proj_ref), (wins_hbm, wins_ref),
        ))
    ]
    for cp in small_inputs:
        cp.start()
    stream_to(flight)

    barrier = pltpu.get_barrier_semaphore()
    for d in range(1, nfeat):
        pl.semaphore_signal(
            barrier, inc=1, device_id=(row, lax.rem(feat + d, nfeat)), device_id_type=MESH
        )
    for d in range(1, nrows):
        pl.semaphore_signal(
            barrier, inc=1, device_id=(lax.rem(row + d, nrows), feat), device_id_type=MESH
        )

    def other(d):
        if chips != 4:
            return lax.rem(chip + d, chips)
        y, x = lax.div(chip, 2), lax.rem(chip, 2)
        return ((y * 2 + 1 - x), ((1 - y) * 2 + x), ((1 - y) * 2 + 1 - x))[d - 1]

    def remote(src, dst, send, recv, to_row, to_feat):
        return pltpu.make_async_remote_copy(
            src_ref=src, dst_ref=dst, send_sem=send, recv_sem=recv,
            device_id=(to_row, to_feat), device_id_type=MESH,
        )

    def push(*args):
        remote(*args).start()

    def arrived(view, recv):
        remote(view, view, recv, recv, partner, feat).wait_recv()

    def all_sent(view, send):
        remote(view, view, send, send, partner, feat).wait_send()

    eye = (
        lax.broadcasted_iota(jnp.int32, (rdim, rdim), 0)
        == lax.broadcasted_iota(jnp.int32, (rdim, rdim), 1)
    ).astype(F32).astype(BF16)
    for cp in small_inputs[:3]:
        cp.wait()
    models3 = jnp.concatenate(split3(models_ref[...]), axis=0)
    models3_t = dot_nt(eye, models3).astype(BF16)

    label = lax.broadcasted_iota(jnp.int32, (nm, SUB), 0)
    for s in range(tokens // SUB):
        at = pl.ds(s * SUB, SUB)
        pick = (
            (label == first_ref[:, at]).astype(F32) - (label == second_ref[:, at]).astype(F32)
        ).astype(BF16)
        pick_v[:, at] = pick
        pick3 = jnp.concatenate([pick, pick, pick], axis=0)
        gap_v[:, at] = jnp.dot(models3_t, pick3, preferred_element_type=F32)
        if s % 6 == 5:
            ready_to(min(s // 6 + 1, 3))

    for cp in small_inputs[3:]:
        cp.wait()
    proj_t = dot_nt(eye, proj_ref[...]).astype(BF16)

    def partial_margins(c):
        for s in range(t // SUB):
            ready_to(((c * t + (s + 1) * SUB - 1) // piece) + 1)
            at = pl.ds(c * t + s * SUB, SUB)
            routed = dot_nt(proj_t, qv[at, :])
            routed_v[:, at] = routed
            marg[feat, :, at] = jnp.sum(routed * gap_v[:, at], axis=0, keepdims=True)

    ends = [chunks * (g + 1) // ngroups for g in range(ngroups)]
    groups = [range(a, b) for a, b in zip([0] + ends[:-1], ends)]

    def cut(g):
        return pl.ds(groups[g].start * t, len(groups[g]) * t)

    for g in range(ngroups):
        for c in groups[g]:
            partial_margins(c)
        if g == 0:
            pl.semaphore_wait(barrier, nfeat - 1 + nrows - 1)
        for d in range(1, nfeat):
            view = marg.at[feat, :, cut(g)]
            push(view, view, mg_s, mg_r.at[g], row, lax.rem(feat + d, nfeat))

    def block_of(i):
        if gpb == 1 and chips == 4:
            return other(3 - i) if i < 3 else chip
        return lax.rem(lax.div(chip, gpb) + 1 + i, blocks)

    def block_part(i, g, acc):
        cols = pl.ds(pl.multiple_of(block_of(i) * bw, 128), bw)
        for c in groups[g]:
            at = pl.ds(c * t, t)
            acc = acc + jnp.dot(back_v[:, at], qv[at, cols], preferred_element_type=F32)
        return acc

    loss_row = jnp.zeros((1, t), F32)
    msum = jnp.zeros((nm, 2 * rdim), F32)
    for g in range(ngroups):
        arrived(marg.at[pl.ds(0, nfeat - 1), :, cut(g)], mg_r.at[g])
        for c in groups[g]:
            at = pl.ds(c * t, t)
            margin = marg[0, :, at]
            for z in range(1, nfeat):
                margin = margin + marg[z, :, at]
            sign = 2.0 * wins_ref[:, at].astype(F32) - 1.0
            x = -sign * margin
            loss_row = loss_row + (jnp.maximum(x, 0.0) + jnp.log1p(jnp.exp(-jnp.abs(x))))
            coef = -sign * jax.nn.sigmoid(x) / total_rows
            for s in range(t // SUB):
                sub = pl.ds(c * t + s * SUB, SUB)
                cs = coef[:, s * SUB:(s + 1) * SUB]
                back_v[:, sub] = (cs * gap_v[:, sub]).astype(BF16)
                w = cs * routed_v[:, sub]
                hi = w.astype(BF16)
                lo = (w - hi.astype(F32)).astype(BF16)
                msum = msum + dot_nt(pick_v[:, sub], jnp.concatenate([hi, lo], axis=0))
        if g < ngroups - 1:
            for i in range(blocks):
                acc = jnp.zeros((rdim, bw), F32) if g == 0 else acc_v[i]
                acc_v[i] = block_part(i, g, acc)

    mbuf[0:nm, :] = msum[:, :rdim] + msum[:, rdim:]
    lsum = loss_row[:, 0:rdim]
    for i in range(1, t // rdim):
        lsum = lsum + loss_row[:, i * rdim:(i + 1) * rdim]
    tail = mbuf.shape[0] - nm
    mbuf[nm:, :] = jnp.where(
        lax.broadcasted_iota(jnp.int32, (tail, rdim), 0) == 0,
        jnp.broadcast_to(lsum, (tail, rdim)), 0.0,
    )
    push(mbuf.at[pl.ds((1 - core) * mh, mh)], mprt, ma_s, ma_r, partner, feat)

    def block_grad(i):
        gblk[i] = block_part(i, ngroups - 1, acc_v[i]).T
        push(gblk.at[i, pl.ds((1 - core) * half, half)], prt.at[i], pr_s, pr_r.at[i], partner, feat)

    def chip_sum(i):
        arrived(prt.at[i], pr_r.at[i])
        csum[i] = gblk[i, pl.ds(core * half, half), :] + prt[i]
        for j in range(gpb):
            to = block_of(i) * gpb + j
            mine = pl.ds(j * fs, fs)

            def send():
                push(csum.at[i, mine], rbuf.at[chip], rs_s, rs_r, to * 2 + core, feat)

            def keep():
                rbuf[chip] = csum[i, mine, :]

            if gpb > 1:
                pl.when(to != chip)(send)
                pl.when(to == chip)(keep)
            elif i < blocks - 1:
                send()
            else:
                keep()

    def models_chip():
        arrived(mprt, ma_r)
        mrow[chip] = mbuf[pl.ds(core * mh, mh), :] + mprt[...]
        for d in range(chips - 1, 0, -1):
            push(mrow.at[chip], mrow.at[chip], mb_s, mb_r, other(d) * 2 + core, feat)

    for i in range(blocks):
        block_grad(i)
        if i == min(2, blocks - 1):
            models_chip()
        if i >= 2:
            chip_sum(i - 2)
    chip_sum(blocks - 2)
    chip_sum(blocks - 1)
    arrived(mrow.at[pl.ds(0, chips - 1)], mb_r)
    mr = mrow[0]
    for i in range(1, chips):
        mr = mr + mrow[i]
    mfeat[feat] = mr
    for d in range(1, nfeat):
        push(mfeat.at[feat], mfeat.at[feat], mc_s, mc_r, row, lax.rem(feat + d, nfeat))

    def slice_of(c, k):
        start = lax.div(c, gpb) * bw + k * half + lax.rem(c, gpb) * fs
        return gfull.at[pl.ds(pl.multiple_of(start, 8), fs)]

    arrived(rbuf.at[pl.ds(0, chips - 1)], rs_r)
    own = rbuf[0]
    for i in range(1, chips):
        own = own + rbuf[i]
    mine = slice_of(chip, core)
    mine[...] = own
    for d in range(chips - 1, 0, -1):
        push(mine, mine, ag_s, ag_r.at[chip], other(d) * 2 + core, feat)
    push(mine, mine, fw_s, fw_r, partner, feat)
    square = own * own
    sq = square[0:8]
    for i in range(1, fs // 8):
        sq = sq + square[i * 8:(i + 1) * 8]
    sqf[feat] = sq
    for d in range(1, nfeat):
        push(sqf.at[feat], sqf.at[feat], sf_s, sf_r, row, lax.rem(feat + d, nfeat))

    arrived(sqf.at[pl.ds(0, nfeat - 1)], sf_r)
    sq = sqf[0]
    for i in range(1, nfeat):
        sq = sq + sqf[i]
    sqr[row] = sq
    for d in range(1, nrows):
        push(sqr.at[row], sqr.at[row], sr_s, sr_r, lax.rem(row + d, nrows), feat)

    arrived(mfeat.at[pl.ds(0, nfeat - 1)], mc_r)
    mt = mfeat[0]
    for i in range(1, nfeat):
        mt = mt + mfeat[i]
    mtot[core] = mt
    push(mtot.at[core], mtot.at[core], md_s, md_r, partner, feat)

    for d in range(1, chips):
        view = slice_of(other(d), core)
        arrived(view, ag_r.at[other(d)])
        push(view, view, fw_s, fw_r, partner, feat)

    all_sent(marg.at[pl.ds(0, nfeat - 1)], mg_s)
    all_sent(mprt, ma_s)
    all_sent(mrow.at[pl.ds(0, chips - 1)], mb_s)
    all_sent(mfeat.at[pl.ds(0, nfeat - 1)], mc_s)
    all_sent(prt, pr_s)
    all_sent(rbuf.at[pl.ds(0, chips - 1)], rs_s)
    all_sent(rbuf.at[pl.ds(0, chips - 1)], ag_s)
    all_sent(sqf.at[pl.ds(0, nfeat - 1)], sf_s)

    arrived(mtot.at[1 - core], md_r)
    grad_models = jnp.concatenate([mtot[0], mtot[1]], axis=0)
    loss = jnp.sum(grad_models[nm:]) / total_rows / float(nfeat)
    grad_models = grad_models[:nm]
    model_square = jnp.sum(grad_models * grad_models)
    small_ref[0:nm] = grad_models
    small_ref[nm + 8:] = jnp.full((8, rdim), loss, F32)
    arrived(sqr.at[pl.ds(0, nrows - 1)], sr_r)
    sq = sqr[0]
    for i in range(1, nrows):
        sq = sq + sqr[i]
    total = jnp.sum(sq) + model_square
    entries = jnp.sqrt(jnp.full((8, rdim), float(total_dim * rdim + nm * rdim), F32))
    small_ref[nm:nm + 8] = entries / (jnp.sqrt(jnp.full((8, rdim), total, F32)) + 1e-06)
    arrived(prt, fw_r)
    out_ref[...] = gfull[...]
    all_sent(mtot.at[0], md_s)
    all_sent(sqr.at[pl.ds(0, nrows - 1)], sr_s)
    all_sent(prt, fw_s)


def finish(nm, grad_ref, small_ref, out_ref, um_ref, loss_ref):
    scale = small_ref[nm:nm + 1, :]
    out_ref[...] = scale * grad_ref[...]
    um_ref[...] = scale * small_ref[0:nm, :]
    loss_ref[0, 0] = small_ref[nm + 8, 0]


def body(queries, projection, models, first, second, wins):
    nrows, nfeat = lax.axis_size("rows"), lax.axis_size("feat")
    tokens, dloc = queries.shape
    rdim = projection.shape[1]
    nm = models.shape[0]
    chips = nrows // 2
    fs = dloc // nrows
    bw = max(2 * fs, 128)
    blocks = dloc // bw
    half = bw // 2
    chunks = tokens // 1024
    mh = (nm + 16) // 2
    vmem = pl.BlockSpec(memory_space=pltpu.VMEM)
    hbm = pl.BlockSpec(memory_space=pl.ANY)
    dma = pltpu.SemaphoreType.DMA
    grad, small = pl.pallas_call(
        functools.partial(kernel, nrows, nfeat, chunks, blocks, dloc * nfeat),
        out_shape=(
            jax.ShapeDtypeStruct((dloc, rdim), F32),
            jax.ShapeDtypeStruct((nm + 16, rdim), F32),
        ),
        in_specs=[hbm] * 6,
        out_specs=(vmem, vmem),
        scratch_shapes=[
            pltpu.VMEM((tokens, dloc), BF16),
            pltpu.VMEM((dloc, rdim), BF16),
            pltpu.VMEM((nm, rdim), F32),
            pltpu.VMEM((1, tokens), jnp.int32),
            pltpu.VMEM((1, tokens), jnp.int32),
            pltpu.VMEM((1, tokens), jnp.int32),
            pltpu.VMEM((rdim, tokens), F32),
            pltpu.VMEM((rdim, tokens), F32),
            pltpu.VMEM((rdim, tokens), BF16),
            pltpu.VMEM((nm, tokens), BF16),
            pltpu.VMEM((nfeat, 1, tokens), F32),
            pltpu.VMEM((blocks, rdim, bw), F32),
            pltpu.VMEM((blocks, bw, rdim), F32),
            pltpu.VMEM((blocks, half, rdim), F32),
            pltpu.VMEM((blocks, half, rdim), F32),
            pltpu.VMEM((chips, fs, rdim), F32),
            pltpu.VMEM((dloc, rdim), F32),
            pltpu.VMEM((2 * mh, rdim), F32),
            pltpu.VMEM((mh, rdim), F32),
            pltpu.VMEM((chips, mh, rdim), F32),
            pltpu.VMEM((nfeat, mh, rdim), F32),
            pltpu.VMEM((2, mh, rdim), F32),
            pltpu.VMEM((nfeat, 8, rdim), F32),
            pltpu.VMEM((nrows, 8, rdim), F32),
            dma((tokens // 512,)), dma((5,)),
            dma, dma((3,)),
            dma, dma((blocks,)),
            dma, dma,
            dma, dma((chips,)),
            dma, dma,
            dma, dma,
            dma, dma,
            dma, dma,
            dma, dma,
            dma, dma,
            dma, dma,
        ],
        compiler_params=pltpu.CompilerParams(
            collective_id=0, has_side_effects=True, vmem_limit_bytes=56 << 20
        ),
    )(
        queries, projection, models,
        first.reshape(1, tokens), second.reshape(1, tokens), wins.reshape(1, tokens),
    )
    out, um, loss = pl.pallas_call(
        functools.partial(finish, nm),
        out_shape=(
            jax.ShapeDtypeStruct((dloc, rdim), F32),
            jax.ShapeDtypeStruct((nm, rdim), F32),
            jax.ShapeDtypeStruct((1, 1), F32),
        ),
        in_specs=[vmem, vmem],
        out_specs=(vmem, vmem, pl.BlockSpec(memory_space=pltpu.SMEM)),
        compiler_params=pltpu.CompilerParams(vmem_limit_bytes=8 << 20),
        name="finish",
    )(grad, small)
    return out, um, loss[0, 0]


def solution(mesh):
    in_specs = (P("rows", "feat"), P("feat", None), P(), P("rows"), P("rows"), P("rows"))
    out_specs = (P("feat", None), P(), P())
    return jax.shard_map(body, mesh=mesh, in_specs=in_specs, out_specs=out_specs, check_vma=False)
```
